512 devices in a mesh: expert: 32 (over y, x), fsdp: 16 (over z, core).
Axes of the slice: x: 4, y: 8, z: 8, core: 2. Of those that a mesh axis runs over, the one named last changes fastest.
Arguments:
- tokens: bfloat16 [4096, 7168], P('expert', 'fsdp'), may hold values from -6 to 6
- counts: int32 [32, 16], P('expert'), may hold values from 1 to 32, as said below
- gate_values: bfloat16 [32, 7168, 1024], P('expert', 'fsdp'), may hold values from -0.0625 to 0.0625
- up_values: bfloat16 [32, 7168, 1024], P('expert', 'fsdp'), may hold values from -0.0625 to 0.0625
- gate_scales: float32 [32, 56, 8], P('expert'), may hold values from 0.5 to 2
- up_scales: float32 [32, 56, 8], P('expert'), may hold values from 0.5 to 2
- grad_hidden: bfloat16 [32, 1024, 1024], P('expert', 'fsdp'), may hold values from -6 to 6
Outputs:
- hidden: bfloat16 [32, 1024, 1024], P('expert', 'fsdp')
- grad_gate: bfloat16 [32, 7168, 1024], P('expert', 'fsdp')
- grad_up: bfloat16 [32, 7168, 1024], P('expert', 'fsdp')
- grad_tokens: bfloat16 [4096, 7168], P('expert', 'fsdp')
The draws below stay inside these ranges and needn't reach their ends.
Inputs may be any that keep to these rules, and one draw needn't show every extreme that they name: Each row of counts sums to 128. In every draw one expert, drawn from the seed, receives exactly 32 rows from every source index.
All inputs are finite; a program needn't handle non-finite values.
Results may differ from the reference program's by a relative error of at most 0.025.
Values may be sent and summed in bfloat16 or wider, within the bound.
A program may use at most 64 MiB of HBM per device.

```python
import math
import jax
import jax.numpy as jnp
from jax import lax

D = 7168
ROWS = 128
EXPERTS = 16
HALF = 1024
CAP = 32
SLOTS = 1024
N_EXPERT = 32
N_FSDP = 16


def draw_counts(key, part):
    capacity = CAP
    hot_key, seat_key = jax.random.split(jax.random.fold_in(key, 11))
    hot_expert = jax.random.randint(hot_key, (), 0, EXPERTS)
    extra_rows = ROWS - capacity - (EXPERTS - 1)
    seat_count = (EXPERTS - 1) * (capacity - 1)

    def one_source(sub_key):
        shuffled = jax.random.permutation(sub_key, seat_count)
        chosen = (shuffled < extra_rows).astype(jnp.int32)
        return chosen.reshape(EXPERTS - 1, capacity - 1).sum(axis=1) + 1
    sub_keys = jax.random.split(seat_key, N_EXPERT)
    others = jax.vmap(one_source)(sub_keys)
    columns = jnp.arange(EXPERTS, dtype=jnp.int32)
    shifted = jnp.clip(columns - (columns > hot_expert).astype(jnp.int32), 0, EXPERTS - 2)
    picked = others[:, shifted]
    return jnp.where(columns[None, :] == hot_expert, capacity, picked).astype(jnp.int32)


def shard_levels(own_key, shape, shards, least, largest):
    def one(position, parts):
        draws = jax.random.uniform(jax.random.fold_in(jax.random.fold_in(own_key, 6), position), (parts,), jnp.float32, least / len(shards), largest / len(shards))
        return jnp.repeat(jnp.exp(draws), shape[position] // parts).reshape((-1,) + (1,) * (len(shape) - position - 1))

    loudness = one(*shards[0])
    for cut in shards[1:]:
        loudness = loudness * one(*cut)
    return loudness


def normal_values(stream_key, shape, deviation, bound, cuts=(), kind=jnp.bfloat16):
    values = jax.random.normal(stream_key, shape, jnp.float32) * deviation
    if len(cuts) > 0:
        values = shard_levels(stream_key, shape, cuts, -0.22, 0.18) * values
    return jnp.clip(values, min=-bound, max=bound).astype(kind)


def setup_inputs(seed: int = 0) -> dict:
    key_list = jax.random.split(jax.random.key(seed), 8)
    return {
        "tokens": normal_values(key_list[0], (N_EXPERT * ROWS, D), 1.0, 6.0, ((0, 32), (1, 16))),
        "counts": draw_counts(jax.random.fold_in(key_list[7], 71), 0),
        "gate_values": normal_values(key_list[2], (2 * EXPERTS, D, HALF), D ** -0.5, 0.0625, ((0, 32), (1, 16))),
        "up_values": normal_values(key_list[3], (2 * EXPERTS, D, HALF), D ** -0.5, 0.0625, ((0, 32), (1, 16))),
        "gate_scales": jnp.clip(jnp.exp(math.log(2.0) - 1.3862944 * jax.random.uniform(key_list[4], (2 * EXPERTS, D // 128, HALF // 128), jnp.float32) ** shard_levels(key_list[4], (2 * EXPERTS, D // 128, HALF // 128), ((0, 32),), -0.2, 0.2)), 0.5, 2.0),
        "up_scales": jnp.clip(jnp.exp(math.log(2.0) - 1.3862944 * jax.random.uniform(key_list[5], (2 * EXPERTS, D // 128, HALF // 128), jnp.float32) ** shard_levels(key_list[5], (2 * EXPERTS, D // 128, HALF // 128), ((0, 32),), -0.2, 0.2)), 0.5, 2.0),
        "grad_hidden": normal_values(key_list[6], (2 * EXPERTS, SLOTS, HALF), 1.0, 6.0, ((0, 32), (1, 16))),
    }


def expand(values, scales):
    grown = jnp.repeat(jnp.repeat(scales, 128, axis=0), 128, axis=1)
    return (values.astype(jnp.float32) * grown).astype(jnp.bfloat16)


def blocked_sum(inputs, weights):
    feat_cols = D // N_FSDP
    slot_count = inputs.shape[0]
    pieces = inputs.reshape(slot_count, N_FSDP, feat_cols).transpose(1, 0, 2)
    blocks = weights.reshape(N_FSDP, feat_cols, weights.shape[1])

    def add_block(running, pair_args):
        in_block, w_block = pair_args
        term_rows = jnp.dot(in_block, w_block, preferred_element_type=jnp.float32).astype(jnp.bfloat16)
        term_rows = lax.optimization_barrier(term_rows)
        return running + term_rows.astype(jnp.float32), None

    running, unused = lax.scan(add_block, jnp.zeros((slot_count, weights.shape[1]), jnp.float32), (pieces, blocks))
    return running


def reference(tokens, counts, gate_values, up_values, gate_scales, up_scales, grad_hidden):
    capacity = CAP
    starts = (jnp.cumsum(counts, axis=1) - counts).astype(jnp.int32)
    slot_ids = jnp.arange(capacity, dtype=jnp.int32)
    source = jnp.arange(N_EXPERT, dtype=jnp.int32)
    spare_row = N_EXPERT * ROWS
    padded = jnp.concatenate([tokens, jnp.zeros((1, D), tokens.dtype)], 0)

    def per_expert(carry, expert):
        live_count = counts[:, expert]
        begin_at = starts[:, expert]
        is_live = slot_ids[None, :] < live_count[:, None]
        gather_ids = jnp.where(is_live, source[:, None] * ROWS + begin_at[:, None] + slot_ids[None, :], spare_row)
        gather_ids = gather_ids.reshape(-1).astype(jnp.int32)
        inputs = padded[gather_ids]
        hiddens, gate_grads, up_grads, backs = [], [], [], []
        for half_id in range(2):
            which = 2 * expert + half_id
            weights = jnp.concatenate([expand(gate_values[which], gate_scales[which]),
                                       expand(up_values[which], up_scales[which])], 1)
            summed = blocked_sum(inputs, weights)
            gate_pre = summed[:, :HALF]
            up_pre = summed[:, HALF:]
            sigmoid_gate = jax.nn.sigmoid(gate_pre)
            hiddens.append((gate_pre * sigmoid_gate * up_pre).astype(jnp.bfloat16))
            cot_rows = grad_hidden[which].astype(jnp.float32)
            grad_gate_pre = (cot_rows * up_pre * sigmoid_gate * (1.0 + gate_pre * (1.0 - sigmoid_gate))).astype(jnp.bfloat16)
            grad_up_pre = (cot_rows * gate_pre * sigmoid_gate).astype(jnp.bfloat16)
            grads = jnp.concatenate([grad_gate_pre, grad_up_pre], 1)
            weight_grad = jnp.dot(inputs.T, grads, preferred_element_type=jnp.float32)
            gate_grads.append(weight_grad[:, :HALF].astype(jnp.bfloat16))
            up_grads.append(weight_grad[:, HALF:].astype(jnp.bfloat16))
            backs.append(jnp.dot(grads, weights.T, preferred_element_type=jnp.float32).astype(jnp.bfloat16))
        combined = (backs[0].astype(jnp.float32) + backs[1].astype(jnp.float32)).astype(jnp.bfloat16)
        carry = carry.at[gather_ids].set(combined)
        return carry, (jnp.stack(hiddens), jnp.stack(gate_grads), jnp.stack(up_grads))

    grad_tokens, stacked = lax.scan(per_expert, jnp.zeros((spare_row + 1, D), jnp.bfloat16),
                                    jnp.arange(EXPERTS, dtype=jnp.int32))
    hidden = stacked[0].reshape(2 * EXPERTS, N_EXPERT * capacity, HALF)
    grad_gate = stacked[1].reshape(2 * EXPERTS, D, HALF)
    grad_up = stacked[2].reshape(2 * EXPERTS, D, HALF)
    return (hidden, grad_gate, grad_up, grad_tokens[:spare_row])
```

```python
import functools

import jax
import jax.numpy as jnp
from jax import lax
from jax.experimental import pallas as pl
from jax.experimental.pallas import tpu as pltpu
from jax.sharding import PartitionSpec as P

MESH = pl.DeviceIdType.MESH
NX, NY, NZ = 4, 8, 8
CAP = 32
EXPERTS = 16
FEAT = 448
HALF = 1024
HH = HALF // 2
CH = NX * CAP
SPLIT = 2
SUB = CH // SPLIT
F32 = jnp.float32
BF16 = jnp.bfloat16
NT = (((1,), (1,)), ((), ()))
TN = (((0,), (0,)), ((), ()))


def rows_of(index, size):
    return pl.ds(pl.multiple_of(index * size, size), size)


def body(
    tok, counts, gv, uv, gs, us, gh,
    hid_o, gg_o, gu_o, gt_o,
    pick, packed, xin, gvb, uvb, wts, pown, psend, precv,
    lsend, lrecv, ssend, srecv, gh2, hid2, hidr, grads, back, backr, comb, ret,
    wsem, ghsem, hsem, xds, xdr, xfs, xfr, pss, psr, lss, lrs, sss, srs,
    als, alr, ass, asr, sbs, sbr, bps, bpr, rts, rtr,
):
    ei = lax.axis_index("expert")
    fi = lax.axis_index("fsdp")
    y, x = ei // NX, ei % NX
    z, c = fi // 2, fi % 2
    p = x // 2
    s = 1 - 2 * c
    xr = NX - 1 - x
    xp = x + 1 - 2 * (x % 2)
    xq = NX - 1 - xp
    partner = y * NX + xp
    sib = fi + s
    nxt = ((z + s + NZ) % NZ) * 2 + c
    prv = ((z - s + NZ) % NZ) * 2 + c

    def chunk(step):
        return (z + s * step + NZ) % NZ

    def send(src, dst, ssem, rsem, expert, fsdp):
        return pltpu.make_async_remote_copy(
            src_ref=src, dst_ref=dst, send_sem=ssem, recv_sem=rsem,
            device_id=(expert, fsdp), device_id_type=MESH,
        )

    barrier = pltpu.get_barrier_semaphore()

    def greet(expert, fsdp):
        pl.semaphore_signal(barrier, inc=1, device_id=(expert, fsdp), device_id_type=MESH)

    greet(ei, sib)
    greet(ei, nxt)
    greet(ei, prv)
    greet(partner, fi)
    for k in range(NY):
        yd = (y + k) % NY
        if k > 0:
            greet(yd * NX + x, fi)
        greet(yd * NX + xr, fi)

    load_g = pltpu.make_async_copy(gv.at[0], gvb, wsem.at[0])
    load_u = pltpu.make_async_copy(uv.at[0], uvb, wsem.at[1])
    load_g.start()
    load_u.start()

    row_id = lax.broadcasted_iota(jnp.int32, (CAP, NX * CAP), 1)
    slot_id = lax.broadcasted_iota(jnp.int32, (CAP, NX * CAP), 0)
    begin = jnp.int32(0)
    for e in range(EXPERTS):
        count = counts[0, e]
        hit = (row_id - begin == slot_id) & (slot_id < count)
        pick[e * CAP:(e + 1) * CAP, :] = jnp.where(hit, 1.0, 0.0).astype(BF16)
        begin = begin + count
    packed[...] = lax.dot_general(
        pick[...], tok[...], NT, preferred_element_type=F32
    ).astype(BF16)

    pl.semaphore_wait(barrier, 2 * NY + 3)

    mine = xin.at[rows_of(ei, CAP), :]

    def dispatch(k, t):
        yd = (y + k) % NY
        expert = 2 * yd + (p if t == 0 else 1 - p)
        return send(
            packed.at[rows_of(expert, CAP), :], mine, xds.at[k, t], xdr.at[y, t],
            yd * NX + (x if t == 0 else xr), fi,
        )

    for k in (4, 3, 5, 2, 6, 1, 7, 0):
        for t in range(2):
            if k > 0 or t > 0:
                dispatch(k, t).start()

    def swap_gh(core):
        return send(
            gh.at[0, :, pl.ds(HH * (1 - core), HH)], gh2.at[core], ghsem.at[0], ghsem.at[1], ei, sib
        )

    for core in range(2):
        @pl.when(c == core)
        def _():
            swap_gh(core).start()
            gh2[core] = gh[0, :, HH * core:HH * (core + 1)]

    own = packed[rows_of(2 * y + p, CAP), :]
    xin[rows_of(ei, CAP), :] = own

    load_g.wait()
    load_u.wait()
    for u in range(7):
        block = (7 * fi + u) // 2
        rows = slice(64 * u, 64 * u + 64)
        for j in range(HALF // 128):
            h, off = j // 4, (j % 4) * 128
            cols = slice(128 * j, 128 * j + 128)
            wts[h, rows, off:off + 128] = (gvb[rows, cols].astype(F32) * gs[j, block]).astype(BF16)
            wts[h, rows, HH + off:HH + off + 128] = (
                uvb[rows, cols].astype(F32) * us[j, block]
            ).astype(BF16)

    def arrived(k, t):
        ys = (y + k) % NY
        src = ys * NX + (x if t == 0 else xr)
        blk = xin.at[rows_of(src, CAP), :]
        return send(blk, blk, xds.at[k, t], xdr.at[ys, t], src, fi)

    def forward(k, t):
        ys = (y + k) % NY
        src = ys * NX + (x if t == 0 else xr)
        blk = xin.at[rows_of(src, CAP), :]
        return send(blk, blk, xfs.at[k, t], xfr.at[ys, t], partner, fi)

    for k in (0, 1, 7, 2, 6, 3, 5, 4):
        for t in range(2):
            if k > 0 or t > 0:
                arrived(k, t).wait_recv()
            forward(k, t).start()

    for k in (0, 1, 7, 2, 6, 3, 5, 4):
        for t in range(2):
            ys = (y + k) % NY
            src = ys * NX + (xp if t == 0 else xq)
            blk = xin.at[rows_of(src, CAP), :]
            send(blk, blk, xfs.at[k, t], xfr.at[ys, t], partner, fi).wait_recv()

    def trade(i):
        return send(psend.at[i], precv.at[i], pss.at[i], psr.at[i], ei, sib)

    def product(i, carry):
        odd, pair = i % 2, i // 2
        off = (1 - odd) * (4 - pair) - odd * (3 - pair)
        there = xin[rows_of(chunk(-off), CH), :]
        here = xin[rows_of(chunk(off), CH), :]
        for t in range(2):
            cols = slice(HH * t, HH * t + HH)
            psend[i, :, cols] = jnp.dot(
                there, wts[1 - c, :, cols], preferred_element_type=F32
            ).astype(BF16)
        trade(i).start()
        for t in range(2):
            cols = slice(HH * t, HH * t + HH)
            pown[i, :, cols] = jnp.dot(here, wts[c, :, cols], preferred_element_type=F32)
        return carry

    def long_hop(k, q):
        rows = pl.ds(q * SUB, SUB)
        return send(lsend.at[k, rows, :], lrecv.at[k, rows, :], lss.at[k, q], lrs.at[k, q], ei, nxt)

    def short_hop(k, q):
        rows = pl.ds(q * SUB, SUB)
        return send(ssend.at[k, rows, :], srecv.at[k, rows, :], sss.at[k, q], srs.at[k, q], ei, prv)

    def pass_on(i):
        k = i // 2
        hop, out, got = (long_hop, lsend, lrecv) if i % 2 == 0 else (short_hop, ssend, srecv)
        trade(i).wait_recv()
        for q in range(SPLIT):
            rows = slice(q * SUB, q * SUB + SUB)
            total = pown[i, rows, :] + precv[i, rows, :].astype(F32)
            if k > 0:
                hop(k - 1, q).wait_recv()
                total = total + got[k - 1, rows, :].astype(F32)
            out[k, rows, :] = total.astype(BF16)
            hop(k, q).start()

    lax.fori_loop(0, 2, product, 0)
    pass_on(0)
    pass_on(1)
    lax.fori_loop(2, 8, product, 0)
    for i in range(2, 7):
        pass_on(i)

    def gather_hop(kind, k, q):
        row = chunk(-k if kind == "long" else k)
        blk = grads.at[c, pl.ds(pl.multiple_of(row * CH + q * SUB, SUB), SUB), :]
        if kind == "long":
            return send(blk, blk, als.at[k, q], alr.at[k, q], ei, nxt)
        return send(blk, blk, ass.at[k, q], asr.at[k, q], ei, prv)

    def share(label, row, q):
        blk = grads.at[c, pl.ds(pl.multiple_of(row * CH + q * SUB, SUB), SUB), :]
        return send(blk, blk, sbs.at[label, q], sbr.at[label, q], ei, sib)

    def shared(label, row, q):
        blk = grads.at[1 - c, pl.ds(pl.multiple_of(row * CH + q * SUB, SUB), SUB), :]
        return send(blk, blk, sbs.at[label, q], sbr.at[label, q], ei, sib)

    swap_gh(0).wait_recv()
    trade(7).wait_recv()
    for q in range(SPLIT):
        rows = slice(q * SUB, q * SUB + SUB)
        total = pown[7, rows, :] + precv[7, rows, :].astype(F32)
        short_hop(2, q).wait_recv()
        total = total + srecv[2, rows, :].astype(F32)
        long_hop(3, q).wait_recv()
        total = total + lrecv[3, rows, :].astype(F32)
        gate, up = total[:, :HH], total[:, HH:]
        sig = jax.nn.sigmoid(gate)
        cot = gh2[:, :, :].reshape(CH, HH)[rows, :].astype(F32)
        place = pl.ds(pl.multiple_of(z * CH + q * SUB, SUB), SUB)
        grads[c, place, :HH] = (cot * up * sig * (1.0 + gate * (1.0 - sig))).astype(BF16)
        grads[c, place, HH:] = (cot * gate * sig).astype(BF16)
        gather_hop("long", 0, q).start()
        gather_hop("short", 0, q).start()
        share(0, z, q).start()
        hid2[rows, :] = (gate * sig * up).astype(BF16)

    swap_h = send(
        hid2.at[pl.ds(pl.multiple_of((1 - c) * 64, 64), 64), :], hidr, hsem.at[0], hsem.at[1], ei, sib
    )
    swap_h.start()

    def to_partner(j, d, t):
        blk = rows_of(d * NX + (xp if t == 0 else xq), CAP)
        return send(back.at[blk, :], backr.at[blk, :], bps.at[j, t], bpr.at[j, t], partner, fi)

    def from_partner(j, d, t):
        blk = rows_of(d * NX + (x if t == 0 else xr), CAP)
        return send(back.at[blk, :], backr.at[blk, :], bps.at[j, t], bpr.at[j, t], partner, fi)

    def back_rows(j, d, label):
        for q in range(SPLIT):
            shared(label, d, q).wait_recv()
        rows = rows_of(d, CH)
        total = lax.dot_general(grads[0, rows, :], wts[0], NT, preferred_element_type=F32)
        total = total + lax.dot_general(grads[1, rows, :], wts[1], NT, preferred_element_type=F32)
        back[rows, :] = total.astype(BF16)
        for t in range(2):
            to_partner(j, d, t).start()

    def give_back(j, d, t):
        blk = rows_of(d * NX + (x if t == 0 else xr), CAP)
        return send(
            comb.at[blk, :], ret.at[rows_of(2 * y + p, CAP), :], rts.at[j, t], rtr.at[y, t],
            d * NX + (x if t == 0 else xr), fi,
        )

    def combine(j, d):
        for t in range(2):
            from_partner(j, d, t).wait_recv()
            blk = rows_of(d * NX + (x if t == 0 else xr), CAP)
            value = (back[blk, :].astype(F32) + backr[blk, :].astype(F32)).astype(BF16)
            if t == 1:
                comb[blk, :] = value
                give_back(j, d, t).start()
            else:
                @pl.when(d == y)
                def _():
                    ret[rows_of(2 * y + p, CAP), :] = value

                @pl.when(d != y)
                def _():
                    comb[blk, :] = value
                    give_back(j, d, t).start()

    steps = [[(0, 0, 0)]]
    for k in range(4):
        step = [(1 + 2 * k, -(k + 1), 5 + k if k < 3 else 4)]
        if k < 3:
            step.append((2 + 2 * k, k + 1, 1 + k))
        steps.append(step)

    for k in range(4):
        for q in range(SPLIT):
            row = chunk(-(k + 1))
            blk = grads.at[c, pl.ds(pl.multiple_of(row * CH + q * SUB, SUB), SUB), :]
            send(blk, blk, als.at[k, q], alr.at[k, q], ei, nxt).wait_recv()
            if k < 3:
                gather_hop("long", k + 1, q).start()
            share(1 + k, row, q).start()
            if k < 3:
                row = chunk(k + 1)
                blk = grads.at[c, pl.ds(pl.multiple_of(row * CH + q * SUB, SUB), SUB), :]
                send(blk, blk, ass.at[k, q], asr.at[k, q], ei, prv).wait_recv()
                if k < 2:
                    gather_hop("short", k + 1, q).start()
                share(5 + k, row, q).start()
        for j, step, label in steps[k]:
            back_rows(j, chunk(step), label)
        if k > 0:
            for j, step, label in steps[k - 1]:
                combine(j, chunk(step))
    for j, step, label in steps[4]:
        back_rows(j, chunk(step), label)
    for st in steps[3:]:
        for j, step, label in st:
            combine(j, chunk(step))

    def weight_grad(i, carry):
        for t in range(4):
            cols = slice(256 * t, 256 * t + 256)
            total = lax.dot_general(
                xin[...], grads[i, :, cols], TN, preferred_element_type=F32
            ).astype(BF16)
            out = gg_o if t < 2 else gu_o
            out[0, :, pl.ds(pl.multiple_of(i * HH + 256 * (t % 2), 256), 256)] = total
        return carry

    lax.fori_loop(0, 2, weight_grad, 0)

    swap_h.wait_recv()
    for core in range(2):
        @pl.when(c == core)
        def _():
            hid_o[0, :, HH * core:HH * (core + 1)] = hid2[64 * core:64 * core + 64, :]
            hid_o[0, :, HH * (1 - core):HH * (2 - core)] = hidr[...]

    for k in range(NY):
        ys = (y + k) % NY
        for t in range(2):
            if k > 0 or t > 0:
                expert = 2 * ys + (p if t == 0 else 1 - p)
                blk = ret.at[rows_of(expert, CAP), :]
                send(blk, blk, rts.at[0, t], rtr.at[ys, t], ys * NX + (x if t == 0 else xr), fi).wait_recv()
    gt_o[...] = lax.dot_general(ret[...], pick[...], TN, preferred_element_type=F32).astype(BF16)

    for k in range(NY):
        for t in range(2):
            if k > 0 or t > 0:
                dispatch(k, t).wait_send()
            forward(k, t).wait_send()
    swap_gh(0).wait_send()
    swap_h.wait_send()
    for i in range(8):
        trade(i).wait_send()
    for q in range(SPLIT):
        for k in range(4):
            long_hop(k, q).wait_send()
            gather_hop("long", k, q).wait_send()
            if k < 3:
                short_hop(k, q).wait_send()
                gather_hop("short", k, q).wait_send()
        for label in range(8):
            share(label, z, q).wait_send()
    for st in steps:
        for j, step, label in st:
            d = chunk(step)
            for t in range(2):
                to_partner(j, d, t).wait_send()
            give_back(j, d, 1).wait_send()

            @pl.when(d != y)
            def _():
                give_back(j, d, 0).wait_send()


def on_device(tokens, counts, gate_values, up_values, gate_scales, up_scales, grad_hidden):
    vmem = pl.BlockSpec(memory_space=pltpu.VMEM)
    smem = pl.BlockSpec(memory_space=pltpu.SMEM)
    hbm = pl.BlockSpec(memory_space=pl.ANY)
    dma = pltpu.SemaphoreType.DMA
    slots = NX * NY * CAP
    hidden, grad_gate, grad_up, grad_tok = pl.pallas_call(
        body,
        out_shape=(
            jax.ShapeDtypeStruct((1, 64, HALF), BF16),
            jax.ShapeDtypeStruct((1, FEAT, HALF), BF16),
            jax.ShapeDtypeStruct((1, FEAT, HALF), BF16),
            jax.ShapeDtypeStruct((FEAT, 128), BF16),
        ),
        in_specs=[vmem, smem, hbm, hbm, smem, smem, vmem],
        out_specs=(vmem, vmem, vmem, vmem),
        scratch_shapes=[
            pltpu.VMEM((EXPERTS * CAP, 128), BF16),
            pltpu.VMEM((EXPERTS * CAP, FEAT), BF16),
            pltpu.VMEM((slots, FEAT), BF16),
            pltpu.VMEM((FEAT, HALF), BF16),
            pltpu.VMEM((FEAT, HALF), BF16),
            pltpu.VMEM((2, FEAT, HALF), BF16),
            pltpu.VMEM((NZ, CH, HALF), F32),
            pltpu.VMEM((NZ, CH, HALF), BF16),
            pltpu.VMEM((NZ, CH, HALF), BF16),
            pltpu.VMEM((4, CH, HALF), BF16),
            pltpu.VMEM((4, CH, HALF), BF16),
            pltpu.VMEM((3, CH, HALF), BF16),
            pltpu.VMEM((3, CH, HALF), BF16),
            pltpu.VMEM((2, 64, HH), BF16),
            pltpu.VMEM((CH, HH), BF16),
            pltpu.VMEM((64, HH), BF16),
            pltpu.VMEM((2, slots, HALF), BF16),
            pltpu.VMEM((slots, FEAT), BF16),
            pltpu.VMEM((slots, FEAT), BF16),
            pltpu.VMEM((slots, FEAT), BF16),
            pltpu.VMEM((EXPERTS * CAP, FEAT), BF16),
            dma((2,)),
            dma((2,)),
            dma((2,)),
            dma((NY, 2)),
            dma((NY, 2)),
            dma((NY, 2)),
            dma((NY, 2)),
            dma((NZ,)),
            dma((NZ,)),
            dma((4, SPLIT)),
            dma((4, SPLIT)),
            dma((3, SPLIT)),
            dma((3, SPLIT)),
            dma((4, SPLIT)),
            dma((4, SPLIT)),
            dma((3, SPLIT)),
            dma((3, SPLIT)),
            dma((NZ, SPLIT)),
            dma((NZ, SPLIT)),
            dma((NZ, 2)),
            dma((NZ, 2)),
            dma((NZ, 2)),
            dma((NY, 2)),
        ],
        compiler_params=pltpu.CompilerParams(collective_id=0, has_side_effects=True),
        name="moe",
    )(
        tokens.T, counts, gate_values, up_values,
        gate_scales[0].T, up_scales[0].T, grad_hidden,
    )
    return hidden, grad_gate, grad_up, grad_tok.T


def solution(mesh):
    in_specs = (
        P("expert", "fsdp"),
        P("expert", None),
        P("expert", "fsdp", None),
        P("expert", "fsdp", None),
        P("expert", None, None),
        P("expert", None, None),
        P("expert", "fsdp", None),
    )
    out_specs = (
        P("expert", "fsdp", None),
        P("expert", "fsdp", None),
        P("expert", "fsdp", None),
        P("expert", "fsdp"),
    )
    return jax.shard_map(
        on_device, mesh=mesh, in_specs=in_specs, out_specs=out_specs, check_vma=False
    )
```

```python
import functools

import jax
import jax.numpy as jnp
from jax import lax
from jax.experimental import pallas as pl
from jax.experimental.pallas import tpu as pltpu
from jax.sharding import PartitionSpec as P

MESH = pl.DeviceIdType.MESH
NX, NY, NZ = 4, 8, 8
CAP = 32
EXPERTS = 16
FEAT = 448
HALF = 1024
HH = HALF // 2
PARTS = 2
PIECE = CAP // PARTS
CH = NX * PIECE
PAIR = 2 * PIECE
SPLIT = 2
SUB = CH // SPLIT
PLACES = (0, 3, 1, 2)
STEPS = (4, -3, 3, -2, 2, -1, 1, 0)
NEAR = (0, 1, 7, 2, 6, 3, 5, 4)
F32 = jnp.float32
BF16 = jnp.bfloat16
NT = (((1,), (1,)), ((), ()))
TN = (((0,), (0,)), ((), ()))


def body(
    tok_h, counts_h, gv, uv, gs_h, us_h, gh_h,
    hid_o, gg_o, gu_o, gt_o,
    counts, gs, us, tok, gh, pick, packed, xin, gvb, uvb, wts, pown, psend, precv,
    lsend, lrecv, ssend, srecv, gh2, hid2, hidr, grads, back, backr, comb, ret,
    wsem, ghsem, hsem, xds, xdr, xfs, xfr, pss, psr, lss, lrs, sss, srs,
    als, alr, ass, asr, sbs, sbr, bps, bpr, rts, rtr,
):
    phase = jax.named_scope
    ei = lax.axis_index("expert")
    fi = lax.axis_index("fsdp")
    y, x = ei // NX, ei % NX
    z, c = fi // 2, fi % 2
    p = x // 2
    g = ((x + 1) // 2) % 2
    s = 1 - 2 * c
    xr = NX - 1 - x
    partner = y * NX + x + 1 - 2 * (x % 2)
    sib = fi + s
    nxt = ((z + s + NZ) % NZ) * 2 + c
    prv = ((z - s + NZ) % NZ) * 2 + c
    parts = range(PARTS)

    def chunk(step):
        return (z + s * step + NZ) % NZ

    def rows(a, d, first=0, size=CH):
        start = (a * NZ + d) * CH + first
        return pl.ds(pl.multiple_of(start, size), size)

    def send(src, dst, ssem, rsem, expert, fsdp):
        return pltpu.make_async_remote_copy(
            src_ref=src, dst_ref=dst, send_sem=ssem, recv_sem=rsem,
            device_id=(expert, fsdp), device_id_type=MESH,
        )

    barrier = pltpu.get_barrier_semaphore()

    def greet(expert, fsdp):
        pl.semaphore_signal(barrier, inc=1, device_id=(expert, fsdp), device_id_type=MESH)

    loads = [
        pltpu.make_async_copy(tok_h, tok, wsem.at[0]),
        pltpu.make_async_copy(gh_h.at[0], gh, wsem.at[1]),
        pltpu.make_async_copy(gv.at[0], gvb, wsem.at[2]),
        pltpu.make_async_copy(uv.at[0], uvb, wsem.at[3]),
        pltpu.make_async_copy(gs_h, gs, wsem.at[4]),
        pltpu.make_async_copy(us_h, us, wsem.at[5]),
        pltpu.make_async_copy(counts_h, counts, wsem.at[6]),
    ]
    with phase("greet"):
        for load in loads:
            load.start()
        for k in (4, 3, 5, 2, 6, 1, 7, 0):
            yd = (y + k) % NY
            if k > 0:
                greet(yd * NX + x, fi)
            greet(yd * NX + xr, fi)
        greet(partner, fi)
        greet(ei, nxt)
        greet(ei, prv)
        greet(ei, sib)

    with phase("pack"):
        row_id = lax.broadcasted_iota(jnp.int32, (CAP, NX * CAP), 1)
        slot_id = lax.broadcasted_iota(jnp.int32, (CAP, NX * CAP), 0)
        begin = jnp.int32(0)
        loads[6].wait()
        for e in range(EXPERTS):
            count = counts[0, e]
            hit = (row_id - begin == slot_id) & (slot_id < count)
            pick[e * CAP:(e + 1) * CAP, :] = jnp.where(hit, 1.0, 0.0).astype(BF16)
            begin = begin + count
        loads[0].wait()
        packed[...] = lax.dot_general(
            pick[...], tok[...], NT, preferred_element_type=F32
        ).astype(BF16)
        loads[1].wait()

    with phase("barrier"):
        pl.semaphore_wait(barrier, 2 * NY + 3)

    def packed_rows(a, expert):
        return pl.ds(pl.multiple_of(expert * CAP + a * PIECE, PIECE), PIECE)

    def dispatch(a, k, t):
        yd = (y + k) % NY
        expert = 2 * yd + (p if t == 0 else 1 - p)
        return send(
            packed.at[packed_rows(a, expert), :],
            xin.at[rows(a, y, (2 * g + p) * PIECE, PIECE), :],
            xds.at[a, k, t], xdr.at[a, y, t], yd * NX + (x if t == 0 else xr), fi,
        )

    def arrived(a, k, t):
        ys = (y + k) % NY
        blk = xin.at[rows(a, ys, (2 * g + (p if t == 0 else 1 - p)) * PIECE, PIECE), :]
        return send(blk, blk, xds.at[a, k, t], xdr.at[a, ys, t], partner, fi)

    def forward(a, k):
        ys = (y + k) % NY
        blk = xin.at[rows(a, ys, g * PAIR, PAIR), :]
        return send(blk, blk, xfs.at[a, k], xfr.at[a, ys], partner, fi)

    def forwarded(a, k):
        ys = (y + k) % NY
        blk = xin.at[rows(a, ys, (1 - g) * PAIR, PAIR), :]
        return send(blk, blk, xfs.at[a, k], xfr.at[a, ys], partner, fi)

    def swap_gh(core):
        return send(
            gh.at[:, pl.ds(HH * (1 - core), HH)], gh2.at[pl.ds(64 * core, 64), :],
            ghsem.at[0], ghsem.at[1], ei, sib,
        )

    with phase("dispatch"):
        for a in parts:
            for k in NEAR:
                for t in range(2):
                    if k > 0 or t > 0:
                        dispatch(a, k, t).start()
        for core in range(2):
            @pl.when(c == core)
            def _():
                swap_gh(core).start()
                gh2[64 * core:64 * core + 64, :] = gh[:, HH * core:HH * (core + 1)]
        for a in parts:
            xin[rows(a, y, (2 * g + p) * PIECE, PIECE), :] = packed[packed_rows(a, 2 * y + p), :]

    with phase("weights"):
        for load in loads[2:6]:
            load.wait()
        for u in range(7):
            block = (7 * fi + u) // 2
            feats = slice(64 * u, 64 * u + 64)
            for j in range(HALF // 128):
                h, off = j // 4, (j % 4) * 128
                cols = slice(128 * j, 128 * j + 128)
                wts[h, feats, off:off + 128] = (
                    gvb[feats, cols].astype(F32) * gs[j, block]
                ).astype(BF16)
                wts[h, feats, HH + off:HH + off + 128] = (
                    uvb[feats, cols].astype(F32) * us[j, block]
                ).astype(BF16)

    def relay(a, ks):
        with phase(f"relay{a}"):
            for k in ks:
                for t in range(2):
                    if k > 0 or t > 0:
                        arrived(a, k, t).wait_recv()
                forward(a, k).start()

    def trade(a, d):
        return send(
            psend.at[rows(a, d), :], precv.at[rows(a, d), :], pss.at[a, d], psr.at[a, d], ei, sib
        )

    def relayed(a):
        with phase(f"relayed{a}"):
            for k in NEAR:
                forwarded(a, k).wait_recv()

    def product(a, half, out):
        def step(i, carry):
            r = pl.ds(pl.multiple_of(a * NZ * CH + 256 * i, 256), 256)
            left = xin[r, :]
            for t in range(4):
                cols = slice(256 * t, 256 * t + 256)
                out[r, cols] = jnp.dot(
                    left, wts[half, :, cols], preferred_element_type=F32
                ).astype(out.dtype)
            return carry

        lax.fori_loop(0, NZ * CH // 256, step, 0)

    def theirs(a):
        with phase(f"theirs{a}"):
            product(a, 1 - c, psend)
            for step in STEPS:
                trade(a, chunk(-step)).start()

    def ours(a):
        with phase(f"ours{a}"):
            product(a, c, pown)

    def hop(a, i, q):
        k = i // 2
        r = pl.ds(q * SUB, SUB)
        if i % 2 == 0:
            return send(
                lsend.at[a, k, r, :], lrecv.at[a, k, r, :], lss.at[a, k, q], lrs.at[a, k, q], ei, nxt
            )
        return send(
            ssend.at[a, k, r, :], srecv.at[a, k, r, :], sss.at[a, k, q], srs.at[a, k, q], ei, prv
        )

    def pass_on(a, i):
        with phase(f"ring{a}_{i}"):
            k, d = i // 2, chunk(STEPS[i])
            out, got = (lsend, lrecv) if i % 2 == 0 else (ssend, srecv)
            trade(a, d).wait_recv()
            for q in range(SPLIT):
                r = slice(q * SUB, q * SUB + SUB)
                src = rows(a, d, q * SUB, SUB)
                total = pown[src, :] + precv[src, :].astype(F32)
                if k > 0:
                    hop(a, i - 2, q).wait_recv()
                    total = total + got[a, k - 1, r, :].astype(F32)
                out[a, k, r, :] = total.astype(BF16)
                hop(a, i, q).start()

    def long_hop(a, k, q):
        blk = grads.at[c, rows(a, chunk(-k), q * SUB, SUB), :]
        return send(blk, blk, als.at[a, k, q], alr.at[a, k, q], ei, nxt)

    def short_hop(a, k, q):
        blk = grads.at[c, rows(a, chunk(k), q * SUB, SUB), :]
        return send(blk, blk, ass.at[a, k, q], asr.at[a, k, q], ei, prv)

    def long_got(a, k, q):
        blk = grads.at[c, rows(a, chunk(-(k + 1)), q * SUB, SUB), :]
        return send(blk, blk, als.at[a, k, q], alr.at[a, k, q], ei, nxt)

    def short_got(a, k, q):
        blk = grads.at[c, rows(a, chunk(k + 1), q * SUB, SUB), :]
        return send(blk, blk, ass.at[a, k, q], asr.at[a, k, q], ei, prv)

    def share(a, label, d):
        blk = grads.at[c, rows(a, d), :]
        return send(blk, blk, sbs.at[a, label], sbr.at[a, label], ei, sib)

    def shared(a, label, d):
        blk = grads.at[1 - c, rows(a, d), :]
        return send(blk, blk, sbs.at[a, label], sbr.at[a, label], ei, sib)

    def activate(a):
        with phase(f"act{a}"):
            trade(a, z).wait_recv()
            for q in range(SPLIT):
                r = slice(q * SUB, q * SUB + SUB)
                src = rows(a, z, q * SUB, SUB)
                total = pown[src, :] + precv[src, :].astype(F32)
                hop(a, 5, q).wait_recv()
                total = total + srecv[a, 2, r, :].astype(F32)
                hop(a, 6, q).wait_recv()
                total = total + lrecv[a, 3, r, :].astype(F32)
                gate, up = total[:, :HH], total[:, HH:]
                sig = jax.nn.sigmoid(gate)
                spots = [
                    CAP * PLACES[i] + PIECE * a
                    for i in range(q * SUB // PIECE, (q + 1) * SUB // PIECE)
                ]
                cot = jnp.concatenate([gh2[i:i + PIECE, :] for i in spots], 0).astype(F32)
                grads[c, src, :HH] = (cot * up * sig * (1.0 + gate * (1.0 - sig))).astype(BF16)
                grads[c, src, HH:] = (cot * gate * sig).astype(BF16)
                long_hop(a, 0, q).start()
                short_hop(a, 0, q).start()
                hidden = (gate * sig * up).astype(BF16)
                for n, i in enumerate(spots):
                    hid2[i:i + PIECE, :] = hidden[n * PIECE:(n + 1) * PIECE, :]
            share(a, 0, z).start()

    def swap_h():
        return send(
            hid2.at[pl.ds(pl.multiple_of((1 - c) * 64, 64), 64), :], hidr,
            hsem.at[0], hsem.at[1], ei, sib,
        )

    def gather(a, k):
        with phase(f"gather{a}_{k}"):
            for q in range(SPLIT):
                long_got(a, k, q).wait_recv()
                if k < 3:
                    long_hop(a, k + 1, q).start()
                if k < 3:
                    short_got(a, k, q).wait_recv()
                    if k < 2:
                        short_hop(a, k + 1, q).start()
            share(a, 1 + k, chunk(-(k + 1))).start()
            if k < 3:
                share(a, 5 + k, chunk(k + 1)).start()

    legs = [[(0, 0, 0)]]
    for k in range(4):
        leg = [(1 + 2 * k, -(k + 1), 5 + k if k < 3 else 4)]
        if k < 3:
            leg.append((2 + 2 * k, k + 1, 1 + k))
        legs.append(leg)

    def to_partner(a, j, d):
        blk = rows(a, d, (1 - g) * PAIR, PAIR)
        return send(back.at[blk, :], backr.at[blk, :], bps.at[a, j], bpr.at[a, j], partner, fi)

    def from_partner(a, j, d):
        blk = rows(a, d, g * PAIR, PAIR)
        return send(back.at[blk, :], backr.at[blk, :], bps.at[a, j], bpr.at[a, j], partner, fi)

    def give_back(a, j, d, t):
        blk = rows(a, d, (2 * g + (p if t == 0 else 1 - p)) * PIECE, PIECE)
        return send(
            comb.at[blk, :], ret.at[packed_rows(a, 2 * y + p), :], rts.at[a, j, t], rtr.at[a, y, t],
            d * NX + (x if t == 0 else xr), fi,
        )

    def back_rows(a, n):
        with phase(f"back{a}_{n}"):
            leg = legs[n]
            for j, step, label in leg:
                shared(a, label, chunk(step)).wait_recv()
            total = None
            for h in range(2):
                left = [grads[h, rows(a, chunk(step)), :] for j, step, label in leg]
                left = left[0] if len(left) == 1 else jnp.concatenate(left, 0)
                term = lax.dot_general(left, wts[h], NT, preferred_element_type=F32)
                total = term if total is None else total + term
            total = total.astype(BF16)
            for i, (j, step, label) in enumerate(leg):
                back[rows(a, chunk(step)), :] = total[i * CH:(i + 1) * CH, :]
                to_partner(a, j, chunk(step)).start()

    def combine(a, n):
        with phase(f"combine{a}_{n}"):
            for j, step, label in legs[n]:
                d = chunk(step)
                from_partner(a, j, d).wait_recv()
                blk = rows(a, d, g * PAIR, PAIR)
                comb[blk, :] = (back[blk, :].astype(F32) + backr[blk, :].astype(F32)).astype(BF16)
                give_back(a, j, d, 1).start()

                @pl.when(d == y)
                def _():
                    ret[packed_rows(a, 2 * y + p), :] = comb[rows(a, d, (2 * g + p) * PIECE, PIECE), :]

                @pl.when(d != y)
                def _():
                    give_back(a, j, d, 0).start()

    def wgrad(h):
        with phase(f"wgrad{h}"):
            for t in range(4):
                cols = slice(256 * t, 256 * t + 256)
                total = lax.dot_general(
                    xin[...], grads[h, :, cols], TN, preferred_element_type=F32
                ).astype(BF16)
                out = gg_o if t < 2 else gu_o
                first = h * HH + 256 * (t % 2)
                out[0, :, first:first + 256] = total

    relay(0, NEAR)
    relay(1, (0, 1, 7))
    relayed(0)
    theirs(0)
    relay(1, (2, 6))
    ours(0)
    relay(1, (3, 5))
    pass_on(0, 0)
    pass_on(0, 1)
    relay(1, (4,))
    pass_on(0, 2)
    pass_on(0, 3)
    relayed(1)
    theirs(1)
    ours(1)
    pass_on(1, 0)
    pass_on(1, 1)
    pass_on(0, 4)
    pass_on(0, 5)
    pass_on(1, 2)
    pass_on(1, 3)
    pass_on(0, 6)
    pass_on(1, 4)
    pass_on(1, 5)
    swap_gh(0).wait_recv()
    activate(0)
    pass_on(1, 6)
    gather(0, 0)
    activate(1)
    swap_h().start()
    back_rows(0, 0)
    gather(0, 1)
    gather(1, 0)
    back_rows(0, 1)
    combine(0, 0)
    back_rows(1, 0)
    gather(0, 2)
    gather(1, 1)
    back_rows(0, 2)
    combine(0, 1)
    back_rows(1, 1)
    combine(1, 0)
    gather(0, 3)
    gather(1, 2)
    back_rows(0, 3)
    combine(0, 2)
    back_rows(1, 2)
    combine(1, 1)
    back_rows(0, 4)
    combine(0, 3)
    gather(1, 3)
    back_rows(1, 3)
    back_rows(1, 4)
    combine(0, 4)
    combine(1, 2)
    combine(1, 3)
    wgrad(0)
    combine(1, 4)
    wgrad(1)
    with phase("hid"):
        swap_h().wait_recv()
        for core in range(2):
            @pl.when(c == core)
            def _():
                hid_o[0, :, HH * core:HH * (core + 1)] = hid2[64 * core:64 * core + 64, :]
                hid_o[0, :, HH * (1 - core):HH * (2 - core)] = hidr[...]

    with phase("retwait"):
        for a in parts:
            for k in NEAR:
                ys = (y + k) % NY
                for t in range(2):
                    if k > 0 or t > 0:
                        blk = ret.at[packed_rows(a, 2 * ys + (p if t == 0 else 1 - p)), :]
                        send(blk, blk, rts.at[a, 0, t], rtr.at[a, ys, t], partner, fi).wait_recv()
    with phase("unpack"):
        gt_o[...] = lax.dot_general(
            ret[...], pick[...], TN, preferred_element_type=F32
        ).astype(BF16)

    swap_gh(0).wait_send()
    swap_h().wait_send()
    for a in parts:
        for k in range(NY):
            for t in range(2):
                if k > 0 or t > 0:
                    dispatch(a, k, t).wait_send()
            forward(a, k).wait_send()
            trade(a, k).wait_send()
            share(a, k, z).wait_send()
        for q in range(SPLIT):
            for i in range(7):
                hop(a, i, q).wait_send()
            for k in range(4):
                long_hop(a, k, q).wait_send()
                if k < 3:
                    short_hop(a, k, q).wait_send()
        for leg in legs:
            for j, step, label in leg:
                d = chunk(step)
                to_partner(a, j, d).wait_send()
                give_back(a, j, d, 1).wait_send()

                @pl.when(d != y)
                def _():
                    give_back(a, j, d, 0).wait_send()


def on_device(tokens, counts, gate_values, up_values, gate_scales, up_scales, grad_hidden):
    vmem = pl.BlockSpec(memory_space=pltpu.VMEM)
    hbm = pl.BlockSpec(memory_space=pltpu.HBM)
    dma = pltpu.SemaphoreType.DMA
    slots = NX * NY * CAP
    hidden, grad_gate, grad_up, grad_tok = pl.pallas_call(
        body,
        out_shape=(
            jax.ShapeDtypeStruct((1, 64, HALF), BF16),
            jax.ShapeDtypeStruct((1, FEAT, HALF), BF16),
            jax.ShapeDtypeStruct((1, FEAT, HALF), BF16),
            jax.ShapeDtypeStruct((FEAT, 128), BF16),
        ),
        in_specs=[hbm] * 7,
        out_specs=(vmem, vmem, vmem, vmem),
        scratch_shapes=[
            pltpu.SMEM((1, EXPERTS), jnp.int32),
            pltpu.SMEM((8, 56), F32),
            pltpu.SMEM((8, 56), F32),
            pltpu.VMEM((FEAT, 128), BF16),
            pltpu.VMEM((64, HALF), BF16),
            pltpu.VMEM((EXPERTS * CAP, 128), BF16),
            pltpu.VMEM((EXPERTS * CAP, FEAT), BF16),
            pltpu.VMEM((slots, FEAT), BF16),
            pltpu.VMEM((FEAT, HALF), BF16),
            pltpu.VMEM((FEAT, HALF), BF16),
            pltpu.VMEM((2, FEAT, HALF), BF16),
            pltpu.VMEM((slots, HALF), F32),
            pltpu.VMEM((slots, HALF), BF16),
            pltpu.VMEM((slots, HALF), BF16),
            pltpu.VMEM((PARTS, 4, CH, HALF), BF16),
            pltpu.VMEM((PARTS, 4, CH, HALF), BF16),
            pltpu.VMEM((PARTS, 3, CH, HALF), BF16),
            pltpu.VMEM((PARTS, 3, CH, HALF), BF16),
            pltpu.VMEM((128, HH), BF16),
            pltpu.VMEM((128, HH), BF16),
            pltpu.VMEM((64, HH), BF16),
            pltpu.VMEM((2, slots, HALF), BF16),
            pltpu.VMEM((slots, FEAT), BF16),
            pltpu.VMEM((slots, FEAT), BF16),
            pltpu.VMEM((slots, FEAT), BF16),
            pltpu.VMEM((EXPERTS * CAP, FEAT), BF16),
            dma((7,)),
            dma((2,)),
            dma((2,)),
            dma((PARTS, NY, 2)),
            dma((PARTS, NY, 2)),
            dma((PARTS, NY)),
            dma((PARTS, NY)),
            dma((PARTS, NZ)),
            dma((PARTS, NZ)),
            dma((PARTS, 4, SPLIT)),
            dma((PARTS, 4, SPLIT)),
            dma((PARTS, 3, SPLIT)),
            dma((PARTS, 3, SPLIT)),
            dma((PARTS, 4, SPLIT)),
            dma((PARTS, 4, SPLIT)),
            dma((PARTS, 3, SPLIT)),
            dma((PARTS, 3, SPLIT)),
            dma((PARTS, NZ)),
            dma((PARTS, NZ)),
            dma((PARTS, NZ)),
            dma((PARTS, NZ)),
            dma((PARTS, NZ, 2)),
            dma((PARTS, NY, 2)),
        ],
        compiler_params=pltpu.CompilerParams(collective_id=0, has_side_effects=True, vmem_limit_bytes=40 << 20),
        name="moe",
    )(
        *(
            pltpu.with_memory_space_constraint(v, pltpu.HBM)
            for v in (
                tokens.T, counts, gate_values, up_values,
                gate_scales[0].T, up_scales[0].T, grad_hidden,
            )
        )
    )
    return hidden, grad_gate, grad_up, grad_tok.T


def solution(mesh):
    in_specs = (
        P("expert", "fsdp"),
        P("expert", None),
        P("expert", "fsdp", None),
        P("expert", "fsdp", None),
        P("expert", None, None),
        P("expert", None, None),
        P("expert", "fsdp", None),
    )
    out_specs = (
        P("expert", "fsdp", None),
        P("expert", "fsdp", None),
        P("expert", "fsdp", None),
        P("expert", "fsdp"),
    )
    return jax.shard_map(
        on_device, mesh=mesh, in_specs=in_specs, out_specs=out_specs, check_vma=False
    )
```

```python
import functools

import jax
import jax.numpy as jnp
from jax import lax
from jax.experimental import pallas as pl
from jax.experimental.pallas import tpu as pltpu
from jax.sharding import PartitionSpec as P

MESH = pl.DeviceIdType.MESH
NX, NY, NZ = 4, 8, 8
CAP = 32
EXPERTS = 16
FEAT = 448
HALF = 1024
HH = HALF // 2
PARTS = 4
PIECE = CAP // PARTS
CH = NX * PIECE
PAIR = 2 * PIECE
SPLIT = 1
SUB = CH // SPLIT
PLACES = (0, 3, 1, 2)
STEPS = (4, -3, 3, -2, 2, -1, 1, 0)
NEAR = (0, 1, 7, 2, 6, 3, 5, 4)
F32 = jnp.float32
BF16 = jnp.bfloat16
NT = (((1,), (1,)), ((), ()))
TN = (((0,), (0,)), ((), ()))


def body(
    tok_h, counts_h, gv, uv, gs_h, us_h, gh_h,
    all_o, gt_o,
    counts, gs, us, tok, gh, pick, packed, xin, gvb, uvb, wts, pown, psend, precv,
    lsend, lrecv, ssend, srecv, gh2, hid2, hidr, grads, back, backr, comb, ret,
    wsem, ghsem, hsem, xds, xdr, xfs, xfr, pss, psr, lss, lrs, sss, srs,
    als, alr, ass, asr, sbs, sbr, bps, bpr, rts, rtr,
):
    phase = jax.named_scope
    ei = lax.axis_index("expert")
    fi = lax.axis_index("fsdp")
    y, x = ei // NX, ei % NX
    z, c = fi // 2, fi % 2
    p = x // 2
    g = ((x + 1) // 2) % 2
    s = 1 - 2 * c
    xr = NX - 1 - x
    partner = y * NX + x + 1 - 2 * (x % 2)
    sib = fi + s
    nxt = ((z + s + NZ) % NZ) * 2 + c
    prv = ((z - s + NZ) % NZ) * 2 + c
    parts = range(PARTS)

    def chunk(step):
        return (z + s * step + NZ) % NZ

    def rows(a, d, first=0, size=CH):
        start = (a * NZ + d) * CH + first
        return pl.ds(pl.multiple_of(start, size), size)

    def send(src, dst, ssem, rsem, expert, fsdp):
        return pltpu.make_async_remote_copy(
            src_ref=src, dst_ref=dst, send_sem=ssem, recv_sem=rsem,
            device_id=(expert, fsdp), device_id_type=MESH,
        )

    barrier = pltpu.get_barrier_semaphore()

    def greet(expert, fsdp):
        pl.semaphore_signal(barrier, inc=1, device_id=(expert, fsdp), device_id_type=MESH)

    loads = [
        pltpu.make_async_copy(tok_h, tok, wsem.at[0]),
        pltpu.make_async_copy(gh_h.at[0], gh, wsem.at[1]),
        pltpu.make_async_copy(gv.at[0], gvb, wsem.at[2]),
        pltpu.make_async_copy(uv.at[0], uvb, wsem.at[3]),
        pltpu.make_async_copy(gs_h, gs, wsem.at[4]),
        pltpu.make_async_copy(us_h, us, wsem.at[5]),
        pltpu.make_async_copy(counts_h, counts, wsem.at[6]),
    ]
    with phase("greet"):
        for load in loads:
            load.start()
        for k in (4, 3, 5, 2, 6, 1, 7, 0):
            yd = (y + k) % NY
            if k > 0:
                greet(yd * NX + x, fi)
            greet(yd * NX + xr, fi)
        greet(partner, fi)
        greet(ei, nxt)
        greet(ei, prv)
        greet(ei, sib)

    with phase("pack"):
        row_id = lax.broadcasted_iota(jnp.int32, (CAP, NX * CAP), 1)
        slot_id = lax.broadcasted_iota(jnp.int32, (CAP, NX * CAP), 0)
        begin = jnp.int32(0)
        loads[6].wait()
        for e in range(EXPERTS):
            count = counts[0, e]
            hit = (row_id - begin == slot_id) & (slot_id < count)
            pick[e * CAP:(e + 1) * CAP, :] = jnp.where(hit, 1.0, 0.0).astype(BF16)
            begin = begin + count
        loads[0].wait()
        packed[...] = lax.dot_general(
            pick[...], tok[...], NT, preferred_element_type=F32
        ).astype(BF16)
        loads[1].wait()

    with phase("barrier"):
        pl.semaphore_wait(barrier, 2 * NY + 3)

    def packed_rows(a, expert):
        return pl.ds(pl.multiple_of(expert * CAP + a * PIECE, PIECE), PIECE)

    def dispatch(a, k, t):
        yd = (y + k) % NY
        expert = 2 * yd + (p if t == 0 else 1 - p)
        return send(
            packed.at[packed_rows(a, expert), :],
            xin.at[rows(a, y, (2 * g + p) * PIECE, PIECE), :],
            xds.at[a, k, t], xdr.at[a, y, t], yd * NX + (x if t == 0 else xr), fi,
        )

    def arrived(a, k, t):
        ys = (y + k) % NY
        blk = xin.at[rows(a, ys, (2 * g + (p if t == 0 else 1 - p)) * PIECE, PIECE), :]
        return send(blk, blk, xds.at[a, k, t], xdr.at[a, ys, t], partner, fi)

    def forward(a, k):
        ys = (y + k) % NY
        blk = xin.at[rows(a, ys, g * PAIR, PAIR), :]
        return send(blk, blk, xfs.at[a, k], xfr.at[a, ys], partner, fi)

    def forwarded(a, k):
        ys = (y + k) % NY
        blk = xin.at[rows(a, ys, (1 - g) * PAIR, PAIR), :]
        return send(blk, blk, xfs.at[a, k], xfr.at[a, ys], partner, fi)

    def swap_gh(core):
        return send(
            gh.at[:, pl.ds(HH * (1 - core), HH)], gh2.at[pl.ds(64 * core, 64), :],
            ghsem.at[0], ghsem.at[1], ei, sib,
        )

    with phase("dispatch"):
        for a in parts:
            for k in NEAR[::-1] if a == 0 else NEAR:
                for t in range(2):
                    if k > 0 or t > 0:
                        dispatch(a, k, t).start()
        for core in range(2):
            @pl.when(c == core)
            def _():
                swap_gh(core).start()
                gh2[64 * core:64 * core + 64, :] = gh[:, HH * core:HH * (core + 1)]
        for a in parts:
            xin[rows(a, y, (2 * g + p) * PIECE, PIECE), :] = packed[packed_rows(a, 2 * y + p), :]

    with phase("weights"):
        for load in loads[2:6]:
            load.wait()
        for u in range(7):
            block = (7 * fi + u) // 2
            feats = slice(64 * u, 64 * u + 64)
            for j in range(HALF // 128):
                h, off = j // 4, (j % 4) * 128
                cols = slice(128 * j, 128 * j + 128)
                wts[h, feats, off:off + 128] = (
                    gvb[feats, cols].astype(F32) * gs[j, block]
                ).astype(BF16)
                wts[h, feats, HH + off:HH + off + 128] = (
                    uvb[feats, cols].astype(F32) * us[j, block]
                ).astype(BF16)

    def relay(a, ks):
        with phase(f"relay{a}"):
            for k in ks:
                for t in range(2):
                    if k > 0 or t > 0:
                        arrived(a, k, t).wait_recv()
                forward(a, k).start()

    def trade(a, d):
        return send(
            psend.at[rows(a, d), :], precv.at[rows(a, d), :], pss.at[a, d], psr.at[a, d], ei, sib
        )

    def relayed(a):
        with phase(f"relayed{a}"):
            for k in NEAR:
                forwarded(a, k).wait_recv()

    def product(a, half, out):
        def step(i, carry):
            r = pl.ds(pl.multiple_of(a * NZ * CH + 256 * i, 256), 256)
            left = xin[r, :]
            for t in range(4):
                cols = slice(256 * t, 256 * t + 256)
                out[r, cols] = jnp.dot(
                    left, wts[half, :, cols], preferred_element_type=F32
                ).astype(out.dtype)
            return carry

        lax.fori_loop(0, NZ * CH // 256, step, 0)

    def theirs(a):
        with phase(f"theirs{a}"):
            product(a, 1 - c, psend)
            for step in STEPS:
                trade(a, chunk(-step)).start()

    def ours(a):
        with phase(f"ours{a}"):
            product(a, c, pown)

    def hop(a, i, q):
        k = i // 2
        r = pl.ds(q * SUB, SUB)
        if i % 2 == 0:
            return send(
                lsend.at[a, k, r, :], lrecv.at[a, k, r, :], lss.at[a, k, q], lrs.at[a, k, q], ei, nxt
            )
        return send(
            ssend.at[a, k, r, :], srecv.at[a, k, r, :], sss.at[a, k, q], srs.at[a, k, q], ei, prv
        )

    def pass_on(a, i):
        with phase(f"ring{a}_{i}"):
            k, d = i // 2, chunk(STEPS[i])
            out, got = (lsend, lrecv) if i % 2 == 0 else (ssend, srecv)
            trade(a, d).wait_recv()
            for q in range(SPLIT):
                r = slice(q * SUB, q * SUB + SUB)
                src = rows(a, d, q * SUB, SUB)
                total = pown[src, :] + precv[src, :].astype(F32)
                if k > 0:
                    hop(a, i - 2, q).wait_recv()
                    total = total + got[a, k - 1, r, :].astype(F32)
                out[a, k, r, :] = total.astype(BF16)
                hop(a, i, q).start()

    def long_hop(a, k, q):
        blk = grads.at[c, rows(a, chunk(-k), q * SUB, SUB), :]
        return send(blk, blk, als.at[a, k, q], alr.at[a, k, q], ei, nxt)

    def short_hop(a, k, q):
        blk = grads.at[c, rows(a, chunk(k), q * SUB, SUB), :]
        return send(blk, blk, ass.at[a, k, q], asr.at[a, k, q], ei, prv)

    def long_got(a, k, q):
        blk = grads.at[c, rows(a, chunk(-(k + 1)), q * SUB, SUB), :]
        return send(blk, blk, als.at[a, k, q], alr.at[a, k, q], ei, nxt)

    def short_got(a, k, q):
        blk = grads.at[c, rows(a, chunk(k + 1), q * SUB, SUB), :]
        return send(blk, blk, ass.at[a, k, q], asr.at[a, k, q], ei, prv)

    def share(a, label, d):
        blk = grads.at[c, rows(a, d), :]
        return send(blk, blk, sbs.at[a, label], sbr.at[a, label], ei, sib)

    def shared(a, label, d):
        blk = grads.at[1 - c, rows(a, d), :]
        return send(blk, blk, sbs.at[a, label], sbr.at[a, label], ei, sib)

    def activate(a):
        with phase(f"act{a}"):
            trade(a, z).wait_recv()
            for q in range(SPLIT):
                r = slice(q * SUB, q * SUB + SUB)
                src = rows(a, z, q * SUB, SUB)
                total = pown[src, :] + precv[src, :].astype(F32)
                hop(a, 5, q).wait_recv()
                total = total + srecv[a, 2, r, :].astype(F32)
                hop(a, 6, q).wait_recv()
                total = total + lrecv[a, 3, r, :].astype(F32)
                gate, up = total[:, :HH], total[:, HH:]
                sig = jax.nn.sigmoid(gate)
                spots = [
                    CAP * PLACES[i] + PIECE * a
                    for i in range(q * SUB // PIECE, (q + 1) * SUB // PIECE)
                ]
                cot = jnp.concatenate([gh2[i:i + PIECE, :] for i in spots], 0).astype(F32)
                grads[c, src, :HH] = (cot * up * sig * (1.0 + gate * (1.0 - sig))).astype(BF16)
                grads[c, src, HH:] = (cot * gate * sig).astype(BF16)
                long_hop(a, 0, q).start()
                short_hop(a, 0, q).start()
                hidden = (gate * sig * up).astype(BF16)
                for n, i in enumerate(spots):
                    hid2[i:i + PIECE, :] = hidden[n * PIECE:(n + 1) * PIECE, :]
            share(a, 0, z).start()

    def swap_h():
        return send(
            hid2.at[pl.ds(pl.multiple_of((1 - c) * 64, 64), 64), :], hidr,
            hsem.at[0], hsem.at[1], ei, sib,
        )

    def gather(a, k):
        with phase(f"gather{a}_{k}"):
            for q in range(SPLIT):
                long_got(a, k, q).wait_recv()
                if k < 3:
                    long_hop(a, k + 1, q).start()
                if k < 3:
                    short_got(a, k, q).wait_recv()
                    if k < 2:
                        short_hop(a, k + 1, q).start()
            share(a, 1 + k, chunk(-(k + 1))).start()
            if k < 3:
                share(a, 5 + k, chunk(k + 1)).start()

    legs = [[(0, 0, 0)]]
    for k in range(4):
        leg = [(1 + 2 * k, -(k + 1), 5 + k if k < 3 else 4)]
        if k < 3:
            leg.append((2 + 2 * k, k + 1, 1 + k))
        legs.append(leg)

    def to_partner(a, j, d):
        blk = rows(a, d, (1 - g) * PAIR, PAIR)
        return send(back.at[blk, :], backr.at[blk, :], bps.at[a, j], bpr.at[a, j], partner, fi)

    def from_partner(a, j, d):
        blk = rows(a, d, g * PAIR, PAIR)
        return send(back.at[blk, :], backr.at[blk, :], bps.at[a, j], bpr.at[a, j], partner, fi)

    def give_back(a, j, d, t):
        blk = rows(a, d, (2 * g + (p if t == 0 else 1 - p)) * PIECE, PIECE)
        return send(
            comb.at[blk, :], ret.at[packed_rows(a, 2 * y + p), :], rts.at[a, j, t], rtr.at[a, y, t],
            d * NX + (x if t == 0 else xr), fi,
        )

    def back_rows(group, n):
        with phase(f"back{group[0]}_{n}"):
            picked = [(a, j, chunk(step), label) for a in group for j, step, label in legs[n]]
            for a, j, d, label in picked:
                shared(a, label, d).wait_recv()
            total = None
            for h in range(2):
                left = [grads[h, rows(a, d), :] for a, j, d, label in picked]
                left = left[0] if len(left) == 1 else jnp.concatenate(left, 0)
                term = lax.dot_general(left, wts[h], NT, preferred_element_type=F32)
                total = term if total is None else total + term
            total = total.astype(BF16)
            for i, (a, j, d, label) in enumerate(picked):
                back[rows(a, d), :] = total[i * CH:(i + 1) * CH, :]
                to_partner(a, j, d).start()

    def combine(group, n):
        with phase(f"combine{group[0]}_{n}"):
            for a in group:
                for j, step, label in legs[n]:
                    combine_one(a, j, chunk(step))

    def combine_one(a, j, d):
        from_partner(a, j, d).wait_recv()
        blk = rows(a, d, g * PAIR, PAIR)
        comb[blk, :] = (back[blk, :].astype(F32) + backr[blk, :].astype(F32)).astype(BF16)
        give_back(a, j, d, 1).start()

        @pl.when(d == y)
        def _():
            ret[packed_rows(a, 2 * y + p), :] = comb[rows(a, d, (2 * g + p) * PIECE, PIECE), :]

        @pl.when(d != y)
        def _():
            give_back(a, j, d, 0).start()

    def wgrad(h):
        with phase(f"wgrad{h}"):
            for t in range(4):
                cols = slice(256 * t, 256 * t + 256)
                total = lax.dot_general(
                    xin[...], grads[h, :, cols], TN, preferred_element_type=F32
                ).astype(BF16)
                top = 0 if t < 2 else FEAT
                first = h * HH + 256 * (t % 2)
                all_o[top:top + FEAT, first:first + 256] = total

    relay(0, (0, 1, 7, 2, 6, 3, 5, 4,))
    relay(1, (0, 1, 7, 2, 6, 3,))
    relayed(0)
    theirs(0)
    relay(1, (5, 4,))
    ours(0)
    relay(2, (0, 1, 7,))
    pass_on(0, 0)
    pass_on(0, 1)
    relay(2, (2, 6, 3,))
    relayed(1)
    theirs(1)
    relay(2, (5, 4,))
    ours(1)
    relay(3, (0, 1, 7,))
    pass_on(0, 2)
    pass_on(0, 3)
    pass_on(1, 0)
    pass_on(1, 1)
    relay(3, (2, 6, 3,))
    relayed(2)
    theirs(2)
    relay(3, (5, 4,))
    ours(2)
    pass_on(0, 4)
    pass_on(0, 5)
    pass_on(2, 0)
    pass_on(2, 1)
    pass_on(1, 2)
    pass_on(1, 3)
    relayed(3)
    theirs(3)
    ours(3)
    pass_on(0, 6)
    pass_on(3, 0)
    pass_on(3, 1)
    pass_on(2, 2)
    pass_on(2, 3)
    pass_on(1, 4)
    pass_on(1, 5)
    swap_gh(0).wait_recv()
    activate(0)
    pass_on(3, 2)
    pass_on(3, 3)
    back_rows((0,), 0)
    pass_on(2, 4)
    pass_on(2, 5)
    pass_on(1, 6)
    combine((0,), 0)
    gather(0, 0)
    pass_on(3, 4)
    pass_on(3, 5)
    back_rows((0,), 1)
    pass_on(2, 6)
    activate(1)
    combine((0,), 1)
    gather(0, 1)
    back_rows((1,), 0)
    pass_on(3, 6)
    back_rows((0,), 2)
    activate(2)
    gather(1, 0)
    combine((1,), 0)
    back_rows((2,), 0)
    combine((0,), 2)
    gather(0, 2)
    back_rows((1,), 1)
    activate(3)
    swap_h().start()
    gather(2, 0)
    back_rows((0,), 3)
    combine((2,), 0)
    back_rows((3,), 0)
    gather(1, 1)
    combine((1,), 1)
    back_rows((2,), 1)
    gather(0, 3)
    combine((0,), 3)
    gather(3, 0)
    back_rows((1,), 2)
    combine((3,), 0)
    back_rows((0,), 4)
    gather(2, 1)
    combine((2,), 1)
    back_rows((3,), 1)
    gather(1, 2)
    combine((1,), 2)
    back_rows((2,), 2)
    gather(3, 1)
    combine((0,), 4)
    back_rows((1,), 3)
    combine((3,), 1)
    gather(2, 2)
    gather(1, 3)
    back_rows((3,), 2)
    combine((2,), 2)
    back_rows((2,), 3)
    combine((1,), 3)
    gather(3, 2)
    back_rows((1,), 4)
    gather(2, 3)
    combine((3,), 2)
    back_rows((3,), 3)
    combine((2,), 3)
    gather(3, 3)
    back_rows((2,), 4)
    combine((1,), 4)
    back_rows((3,), 4)
    combine((3,), 3)
    combine((2,), 4)
    combine((3,), 4)
    wgrad(0)
    wgrad(1)

    with phase("hid"):
        swap_h().wait_recv()
        for core in range(2):
            @pl.when(c == core)
            def _():
                all_o[2 * FEAT:, HH * core:HH * (core + 1)] = hid2[64 * core:64 * core + 64, :]
                all_o[2 * FEAT:, HH * (1 - core):HH * (2 - core)] = hidr[...]

    with phase("retwait"):
        for a in parts:
            for k in NEAR:
                ys = (y + k) % NY
                for t in range(2):
                    if k > 0 or t > 0:
                        blk = ret.at[packed_rows(a, 2 * ys + (p if t == 0 else 1 - p)), :]
                        send(blk, blk, rts.at[a, 0, t], rtr.at[a, ys, t], partner, fi).wait_recv()
    with phase("unpack"):
        gt_o[...] = lax.dot_general(
            ret[...], pick[...], TN, preferred_element_type=F32
        ).astype(BF16)

    swap_gh(0).wait_send()
    swap_h().wait_send()
    for a in parts:
        for k in range(NY):
            for t in range(2):
                if k > 0 or t > 0:
                    dispatch(a, k, t).wait_send()
            forward(a, k).wait_send()
            trade(a, k).wait_send()
            share(a, k, z).wait_send()
        for q in range(SPLIT):
            for i in range(7):
                hop(a, i, q).wait_send()
            for k in range(4):
                long_hop(a, k, q).wait_send()
                if k < 3:
                    short_hop(a, k, q).wait_send()
        for leg in legs:
            for j, step, label in leg:
                d = chunk(step)
                to_partner(a, j, d).wait_send()
                give_back(a, j, d, 1).wait_send()

                @pl.when(d != y)
                def _():
                    give_back(a, j, d, 0).wait_send()


def on_device(tokens, counts, gate_values, up_values, gate_scales, up_scales, grad_hidden):
    vmem = pl.BlockSpec(memory_space=pltpu.VMEM)
    hbm = pl.BlockSpec(memory_space=pltpu.HBM)
    dma = pltpu.SemaphoreType.DMA
    slots = NX * NY * CAP
    packed_out, grad_tok = pl.pallas_call(
        body,
        out_shape=(
            jax.ShapeDtypeStruct((2 * FEAT + 64, HALF), BF16),
            jax.ShapeDtypeStruct((FEAT, 128), BF16),
        ),
        in_specs=[hbm] * 7,
        out_specs=(vmem, vmem),
        scratch_shapes=[
            pltpu.SMEM((1, EXPERTS), jnp.int32),
            pltpu.SMEM((8, 56), F32),
            pltpu.SMEM((8, 56), F32),
            pltpu.VMEM((FEAT, 128), BF16),
            pltpu.VMEM((64, HALF), BF16),
            pltpu.VMEM((EXPERTS * CAP, 128), BF16),
            pltpu.VMEM((EXPERTS * CAP, FEAT), BF16),
            pltpu.VMEM((slots, FEAT), BF16),
            pltpu.VMEM((FEAT, HALF), BF16),
            pltpu.VMEM((FEAT, HALF), BF16),
            pltpu.VMEM((2, FEAT, HALF), BF16),
            pltpu.VMEM((slots, HALF), F32),
            pltpu.VMEM((slots, HALF), BF16),
            pltpu.VMEM((slots, HALF), BF16),
            pltpu.VMEM((PARTS, 4, CH, HALF), BF16),
            pltpu.VMEM((PARTS, 4, CH, HALF), BF16),
            pltpu.VMEM((PARTS, 3, CH, HALF), BF16),
            pltpu.VMEM((PARTS, 3, CH, HALF), BF16),
            pltpu.VMEM((128, HH), BF16),
            pltpu.VMEM((128, HH), BF16),
            pltpu.VMEM((64, HH), BF16),
            pltpu.VMEM((2, slots, HALF), BF16),
            pltpu.VMEM((slots, FEAT), BF16),
            pltpu.VMEM((slots, FEAT), BF16),
            pltpu.VMEM((slots, FEAT), BF16),
            pltpu.VMEM((EXPERTS * CAP, FEAT), BF16),
            dma((7,)),
            dma((2,)),
            dma((2,)),
            dma((PARTS, NY, 2)),
            dma((PARTS, NY, 2)),
            dma((PARTS, NY)),
            dma((PARTS, NY)),
            dma((PARTS, NZ)),
            dma((PARTS, NZ)),
            dma((PARTS, 4, SPLIT)),
            dma((PARTS, 4, SPLIT)),
            dma((PARTS, 3, SPLIT)),
            dma((PARTS, 3, SPLIT)),
            dma((PARTS, 4, SPLIT)),
            dma((PARTS, 4, SPLIT)),
            dma((PARTS, 3, SPLIT)),
            dma((PARTS, 3, SPLIT)),
            dma((PARTS, NZ)),
            dma((PARTS, NZ)),
            dma((PARTS, NZ)),
            dma((PARTS, NZ)),
            dma((PARTS, NZ, 2)),
            dma((PARTS, NY, 2)),
        ],
        compiler_params=pltpu.CompilerParams(collective_id=0, has_side_effects=True, vmem_limit_bytes=40 << 20),
        name="moe",
    )(
        *(
            pltpu.with_memory_space_constraint(v, pltpu.HBM)
            for v in (
                tokens.T, counts, gate_values, up_values,
                gate_scales[0].T, up_scales[0].T, grad_hidden,
            )
        )
    )
    grad_gate = packed_out[None, :FEAT]
    grad_up = packed_out[None, FEAT:2 * FEAT]
    hidden = packed_out[None, 2 * FEAT:]
    return hidden, grad_gate, grad_up, grad_tok.T


def solution(mesh):
    in_specs = (
        P("expert", "fsdp"),
        P("expert", None),
        P("expert", "fsdp", None),
        P("expert", "fsdp", None),
        P("expert", None, None),
        P("expert", None, None),
        P("expert", "fsdp", None),
    )
    out_specs = (
        P("expert", "fsdp", None),
        P("expert", "fsdp", None),
        P("expert", "fsdp", None),
        P("expert", "fsdp"),
    )
    return jax.shard_map(
        on_device, mesh=mesh, in_specs=in_specs, out_specs=out_specs, check_vma=False
    )
```

```python
import functools

import jax
import jax.numpy as jnp
from jax import lax
from jax.experimental import pallas as pl
from jax.experimental.pallas import tpu as pltpu
from jax.sharding import PartitionSpec as P

MESH = pl.DeviceIdType.MESH
NX, NY, NZ = 4, 8, 8
CAP = 32
EXPERTS = 16
FEAT = 448
HALF = 1024
HH = HALF // 2
PARTS = 4
PIECE = CAP // PARTS
CH = NX * PIECE
PAIR = 2 * PIECE
SPLIT = 1
SUB = CH // SPLIT
PLACES = (0, 3, 1, 2)
STEPS = (4, -3, 3, -2, 2, -1, 1, 0)
NEAR = (0, 1, 7, 2, 6, 3, 5, 4)
F32 = jnp.float32
BF16 = jnp.bfloat16
NT = (((1,), (1,)), ((), ()))
TN = (((0,), (0,)), ((), ()))


def body(
    tok_h, counts_h, gv, uv, gs_h, us_h, gh_h,
    all_o, gt_o,
    counts, gs, us, tok, gh, pick, packed, xin, gvb, uvb, wts, pown, psend, precv,
    lsend, lrecv, ssend, srecv, gh2, hid2, hidr, grads, back, backr, comb, ret, early,
    wsem, ghsem, hsem, xds, xdr, xfs, xfr, pss, psr, lss, lrs, sss, srs,
    als, alr, ass, asr, sbs, sbr, bps, bpr, rts, rtr,
):
    phase = jax.named_scope
    ei = lax.axis_index("expert")
    fi = lax.axis_index("fsdp")
    y, x = ei // NX, ei % NX
    z, c = fi // 2, fi % 2
    p = x // 2
    g = ((x + 1) // 2) % 2
    s = 1 - 2 * c
    xr = NX - 1 - x
    partner = y * NX + x + 1 - 2 * (x % 2)
    sib = fi + s
    nxt = ((z + s + NZ) % NZ) * 2 + c
    prv = ((z - s + NZ) % NZ) * 2 + c
    parts = range(PARTS)

    def chunk(step):
        return (z + s * step + NZ) % NZ

    def rows(a, d, first=0, size=CH):
        start = (a * NZ + d) * CH + first
        return pl.ds(pl.multiple_of(start, size), size)

    def send(src, dst, ssem, rsem, expert, fsdp):
        return pltpu.make_async_remote_copy(
            src_ref=src, dst_ref=dst, send_sem=ssem, recv_sem=rsem,
            device_id=(expert, fsdp), device_id_type=MESH,
        )

    barrier = pltpu.get_barrier_semaphore()

    def greet(expert, fsdp):
        pl.semaphore_signal(barrier, inc=1, device_id=(expert, fsdp), device_id_type=MESH)

    loads = [
        pltpu.make_async_copy(tok_h, tok, wsem.at[0]),
        pltpu.make_async_copy(gh_h.at[0], gh, wsem.at[1]),
        pltpu.make_async_copy(gv.at[0], gvb, wsem.at[2]),
        pltpu.make_async_copy(uv.at[0], uvb, wsem.at[3]),
        pltpu.make_async_copy(gs_h, gs, wsem.at[4]),
        pltpu.make_async_copy(us_h, us, wsem.at[5]),
        pltpu.make_async_copy(counts_h, counts, wsem.at[6]),
    ]
    with phase("greet"):
        for load in loads:
            load.start()
        for k in (4, 3, 5, 2, 6, 1, 7, 0):
            yd = (y + k) % NY
            if k > 0:
                greet(yd * NX + x, fi)
            greet(yd * NX + xr, fi)
        greet(partner, fi)
        greet(ei, nxt)
        greet(ei, prv)
        greet(ei, sib)

    with phase("pack"):
        row_id = lax.broadcasted_iota(jnp.int32, (CAP, NX * CAP), 1)
        slot_id = lax.broadcasted_iota(jnp.int32, (CAP, NX * CAP), 0)
        begin = jnp.int32(0)
        loads[6].wait()
        for e in range(EXPERTS):
            count = counts[0, e]
            hit = (row_id - begin == slot_id) & (slot_id < count)
            pick[e * CAP:(e + 1) * CAP, :] = jnp.where(hit, 1.0, 0.0).astype(BF16)
            begin = begin + count
        loads[0].wait()
        packed[...] = lax.dot_general(
            pick[...], tok[...], NT, preferred_element_type=F32
        ).astype(BF16)
        loads[1].wait()

    with phase("barrier"):
        pl.semaphore_wait(barrier, 2 * NY + 3)

    def packed_rows(a, expert):
        return pl.ds(pl.multiple_of(expert * CAP + a * PIECE, PIECE), PIECE)

    def dispatch(a, k, t):
        yd = (y + k) % NY
        expert = 2 * yd + (p if t == 0 else 1 - p)
        return send(
            packed.at[packed_rows(a, expert), :],
            xin.at[rows(a, y, (2 * g + p) * PIECE, PIECE), :],
            xds.at[a, k, t], xdr.at[a, y, t], yd * NX + (x if t == 0 else xr), fi,
        )

    def arrived(a, k, t):
        ys = (y + k) % NY
        blk = xin.at[rows(a, ys, (2 * g + (p if t == 0 else 1 - p)) * PIECE, PIECE), :]
        return send(blk, blk, xds.at[a, k, t], xdr.at[a, ys, t], partner, fi)

    def forward(a, k):
        ys = (y + k) % NY
        blk = xin.at[rows(a, ys, g * PAIR, PAIR), :]
        return send(blk, blk, xfs.at[a, k], xfr.at[a, ys], partner, fi)

    def forwarded(a, k):
        ys = (y + k) % NY
        blk = xin.at[rows(a, ys, (1 - g) * PAIR, PAIR), :]
        return send(blk, blk, xfs.at[a, k], xfr.at[a, ys], partner, fi)

    def swap_gh(core):
        return send(
            gh.at[:, pl.ds(HH * (1 - core), HH)], gh2.at[pl.ds(64 * core, 64), :],
            ghsem.at[0], ghsem.at[1], ei, sib,
        )

    with phase("dispatch"):
        for a in parts:
            for k in NEAR[::-1] if a == 0 else NEAR:
                for t in range(2):
                    if k > 0 or t > 0:
                        dispatch(a, k, t).start()
        for core in range(2):
            @pl.when(c == core)
            def _():
                swap_gh(core).start()
                gh2[64 * core:64 * core + 64, :] = gh[:, HH * core:HH * (core + 1)]
        for a in parts:
            xin[rows(a, y, (2 * g + p) * PIECE, PIECE), :] = packed[packed_rows(a, 2 * y + p), :]

    with phase("weights"):
        for load in loads[2:6]:
            load.wait()
        for u in range(7):
            block = (7 * fi + u) // 2
            feats = slice(64 * u, 64 * u + 64)
            for j in range(HALF // 128):
                h, off = j // 4, (j % 4) * 128
                cols = slice(128 * j, 128 * j + 128)
                wts[h, feats, off:off + 128] = (
                    gvb[feats, cols].astype(F32) * gs[j, block]
                ).astype(BF16)
                wts[h, feats, HH + off:HH + off + 128] = (
                    uvb[feats, cols].astype(F32) * us[j, block]
                ).astype(BF16)

    def relay(a, ks):
        with phase(f"relay{a}"):
            for k in ks:
                for t in range(2):
                    if k > 0 or t > 0:
                        arrived(a, k, t).wait_recv()
                forward(a, k).start()

    def trade(a, d):
        return send(
            psend.at[rows(a, d), :], precv.at[rows(a, d), :], pss.at[a, d], psr.at[a, d], ei, sib
        )

    def relayed(a):
        with phase(f"relayed{a}"):
            for k in NEAR:
                forwarded(a, k).wait_recv()

    def product(a, half, out):
        def step(i, carry):
            r = pl.ds(pl.multiple_of(a * NZ * CH + 256 * i, 256), 256)
            left = xin[r, :]
            for t in range(4):
                cols = slice(256 * t, 256 * t + 256)
                out[r, cols] = jnp.dot(
                    left, wts[half, :, cols], preferred_element_type=F32
                ).astype(out.dtype)
            return carry

        lax.fori_loop(0, NZ * CH // 256, step, 0)

    def theirs(a):
        with phase(f"theirs{a}"):
            product(a, 1 - c, psend)
            for step in STEPS:
                trade(a, chunk(-step)).start()

    def ours(a):
        with phase(f"ours{a}"):
            product(a, c, pown)

    def hop(a, i, q):
        k = i // 2
        r = pl.ds(q * SUB, SUB)
        if i % 2 == 0:
            return send(
                lsend.at[a, k, r, :], lrecv.at[a, k, r, :], lss.at[a, k, q], lrs.at[a, k, q], ei, nxt
            )
        return send(
            ssend.at[a, k, r, :], srecv.at[a, k, r, :], sss.at[a, k, q], srs.at[a, k, q], ei, prv
        )

    def pass_on(a, i):
        with phase(f"ring{a}_{i}"):
            k, d = i // 2, chunk(STEPS[i])
            out, got = (lsend, lrecv) if i % 2 == 0 else (ssend, srecv)
            trade(a, d).wait_recv()
            for q in range(SPLIT):
                r = slice(q * SUB, q * SUB + SUB)
                src = rows(a, d, q * SUB, SUB)
                total = pown[src, :] + precv[src, :].astype(F32)
                if k > 0:
                    hop(a, i - 2, q).wait_recv()
                    total = total + got[a, k - 1, r, :].astype(F32)
                out[a, k, r, :] = total.astype(BF16)
                hop(a, i, q).start()

    def long_hop(a, k, q):
        blk = grads.at[c, rows(a, chunk(-k), q * SUB, SUB), :]
        return send(blk, blk, als.at[a, k, q], alr.at[a, k, q], ei, nxt)

    def short_hop(a, k, q):
        blk = grads.at[c, rows(a, chunk(k), q * SUB, SUB), :]
        return send(blk, blk, ass.at[a, k, q], asr.at[a, k, q], ei, prv)

    def long_got(a, k, q):
        blk = grads.at[c, rows(a, chunk(-(k + 1)), q * SUB, SUB), :]
        return send(blk, blk, als.at[a, k, q], alr.at[a, k, q], ei, nxt)

    def short_got(a, k, q):
        blk = grads.at[c, rows(a, chunk(k + 1), q * SUB, SUB), :]
        return send(blk, blk, ass.at[a, k, q], asr.at[a, k, q], ei, prv)

    def share(a, label, d):
        blk = grads.at[c, rows(a, d), :]
        return send(blk, blk, sbs.at[a, label], sbr.at[a, label], ei, sib)

    def shared(a, label, d):
        blk = grads.at[1 - c, rows(a, d), :]
        return send(blk, blk, sbs.at[a, label], sbr.at[a, label], ei, sib)

    def activate(a):
        with phase(f"act{a}"):
            trade(a, z).wait_recv()
            for q in range(SPLIT):
                r = slice(q * SUB, q * SUB + SUB)
                src = rows(a, z, q * SUB, SUB)
                total = pown[src, :] + precv[src, :].astype(F32)
                hop(a, 5, q).wait_recv()
                total = total + srecv[a, 2, r, :].astype(F32)
                hop(a, 6, q).wait_recv()
                total = total + lrecv[a, 3, r, :].astype(F32)
                gate, up = total[:, :HH], total[:, HH:]
                sig = jax.nn.sigmoid(gate)
                spots = [
                    CAP * PLACES[i] + PIECE * a
                    for i in range(q * SUB // PIECE, (q + 1) * SUB // PIECE)
                ]
                cot = jnp.concatenate([gh2[i:i + PIECE, :] for i in spots], 0).astype(F32)
                grads[c, src, :HH] = (cot * up * sig * (1.0 + gate * (1.0 - sig))).astype(BF16)
                grads[c, src, HH:] = (cot * gate * sig).astype(BF16)
                long_hop(a, 0, q).start()
                short_hop(a, 0, q).start()
                hidden = (gate * sig * up).astype(BF16)
                for n, i in enumerate(spots):
                    hid2[i:i + PIECE, :] = hidden[n * PIECE:(n + 1) * PIECE, :]
            share(a, 0, z).start()

    def swap_h():
        return send(
            hid2.at[pl.ds(pl.multiple_of((1 - c) * 64, 64), 64), :], hidr,
            hsem.at[0], hsem.at[1], ei, sib,
        )

    def gather(a, k):
        with phase(f"gather{a}_{k}"):
            for q in range(SPLIT):
                long_got(a, k, q).wait_recv()
                if k < 3:
                    long_hop(a, k + 1, q).start()
                if k < 3:
                    short_got(a, k, q).wait_recv()
                    if k < 2:
                        short_hop(a, k + 1, q).start()
            share(a, 1 + k, chunk(-(k + 1))).start()
            if k < 3:
                share(a, 5 + k, chunk(k + 1)).start()

    legs = [[(0, 0, 0)]]
    for k in range(4):
        leg = [(1 + 2 * k, -(k + 1), 5 + k if k < 3 else 4)]
        if k < 3:
            leg.append((2 + 2 * k, k + 1, 1 + k))
        legs.append(leg)

    def to_partner(a, j, d):
        blk = rows(a, d, (1 - g) * PAIR, PAIR)
        return send(back.at[blk, :], backr.at[blk, :], bps.at[a, j], bpr.at[a, j], partner, fi)

    def from_partner(a, j, d):
        blk = rows(a, d, g * PAIR, PAIR)
        return send(back.at[blk, :], backr.at[blk, :], bps.at[a, j], bpr.at[a, j], partner, fi)

    def give_back(a, j, d, t):
        blk = rows(a, d, (2 * g + (p if t == 0 else 1 - p)) * PIECE, PIECE)
        return send(
            comb.at[blk, :], ret.at[packed_rows(a, 2 * y + p), :], rts.at[a, j, t], rtr.at[a, y, t],
            d * NX + (x if t == 0 else xr), fi,
        )

    def back_rows(group, n):
        with phase(f"back{group[0]}_{n}"):
            picked = [(a, j, chunk(step), label) for a in group for j, step, label in legs[n]]
            for a, j, d, label in picked:
                shared(a, label, d).wait_recv()
            total = None
            for h in range(2):
                left = [grads[h, rows(a, d), :] for a, j, d, label in picked]
                left = left[0] if len(left) == 1 else jnp.concatenate(left, 0)
                term = lax.dot_general(left, wts[h], NT, preferred_element_type=F32)
                total = term if total is None else total + term
            total = total.astype(BF16)
            for i, (a, j, d, label) in enumerate(picked):
                back[rows(a, d), :] = total[i * CH:(i + 1) * CH, :]
                to_partner(a, j, d).start()

    def combine(group, n):
        with phase(f"combine{group[0]}_{n}"):
            for a in group:
                for j, step, label in legs[n]:
                    combine_one(a, j, chunk(step))

    def combine_one(a, j, d):
        from_partner(a, j, d).wait_recv()
        blk = rows(a, d, g * PAIR, PAIR)
        comb[blk, :] = (back[blk, :].astype(F32) + backr[blk, :].astype(F32)).astype(BF16)
        give_back(a, j, d, 1).start()

        @pl.when(d == y)
        def _():
            ret[packed_rows(a, 2 * y + p), :] = comb[rows(a, d, (2 * g + p) * PIECE, PIECE), :]

        @pl.when(d != y)
        def _():
            give_back(a, j, d, 0).start()

    def wgrad_early(h):
        for t in range(4):
            cols = slice(256 * t, 256 * t + 256)
            early[h, :, cols] = lax.dot_general(
                xin[:512, :], grads[h, :512, cols], TN, preferred_element_type=F32
            )

    def wgrad(h):
        with phase(f"wgrad{h}"):
            for t in range(4):
                cols = slice(256 * t, 256 * t + 256)
                total = early[h, :, cols] + lax.dot_general(
                    xin[512:, :], grads[h, 512:, cols], TN, preferred_element_type=F32
                )
                total = total.astype(BF16)
                top = 0 if t < 2 else FEAT
                first = h * HH + 256 * (t % 2)
                all_o[top:top + FEAT, first:first + 256] = total

    relay(0, (0, 1, 7, 2, 6, 3, 5, 4,))
    relay(1, (0, 1, 7, 2, 6, 3,))
    relayed(0)
    theirs(0)
    relay(1, (5, 4,))
    ours(0)
    relay(2, (0, 1, 7,))
    pass_on(0, 0)
    pass_on(0, 1)
    relay(2, (2, 6, 3,))
    relayed(1)
    theirs(1)
    relay(2, (5, 4,))
    ours(1)
    relay(3, (0, 1, 7,))
    pass_on(0, 2)
    pass_on(0, 3)
    pass_on(1, 0)
    pass_on(1, 1)
    relay(3, (2, 6, 3,))
    relayed(2)
    theirs(2)
    relay(3, (5, 4,))
    ours(2)
    pass_on(0, 4)
    pass_on(0, 5)
    pass_on(2, 0)
    pass_on(2, 1)
    pass_on(1, 2)
    pass_on(1, 3)
    relayed(3)
    theirs(3)
    ours(3)
    pass_on(0, 6)
    pass_on(3, 0)
    pass_on(3, 1)
    pass_on(2, 2)
    pass_on(2, 3)
    pass_on(1, 4)
    pass_on(1, 5)
    swap_gh(0).wait_recv()
    activate(0)
    pass_on(3, 2)
    pass_on(3, 3)
    back_rows((0,), 0)
    pass_on(2, 4)
    pass_on(2, 5)
    pass_on(1, 6)
    combine((0,), 0)
    gather(0, 0)
    pass_on(3, 4)
    pass_on(3, 5)
    back_rows((0,), 1)
    pass_on(2, 6)
    activate(1)
    combine((0,), 1)
    gather(0, 1)
    back_rows((1,), 0)
    pass_on(3, 6)
    back_rows((0,), 2)
    activate(2)
    gather(1, 0)
    combine((1,), 0)
    back_rows((2,), 0)
    combine((0,), 2)
    gather(0, 2)
    back_rows((1,), 1)
    activate(3)
    swap_h().start()
    gather(2, 0)
    back_rows((0,), 3)
    combine((2,), 0)
    back_rows((3,), 0)
    gather(1, 1)
    combine((1,), 1)
    back_rows((2,), 1)
    gather(0, 3)
    combine((0,), 3)
    gather(3, 0)
    back_rows((1,), 2)
    combine((3,), 0)
    back_rows((0,), 4)
    gather(2, 1)
    combine((2,), 1)
    back_rows((3,), 1)
    gather(1, 2)
    combine((1,), 2)
    back_rows((2,), 2)
    gather(3, 1)
    combine((0,), 4)
    back_rows((1,), 3)
    combine((3,), 1)
    gather(2, 2)
    gather(1, 3)
    back_rows((3,), 2)
    combine((2,), 2)
    back_rows((2,), 3)
    combine((1,), 3)
    gather(3, 2)
    back_rows((1,), 4)
    gather(2, 3)
    combine((3,), 2)
    back_rows((3,), 3)
    combine((2,), 3)
    wgrad_early(0)
    gather(3, 3)
    back_rows((2,), 4)
    combine((1,), 4)
    back_rows((3,), 4)
    combine((3,), 3)
    combine((2,), 4)
    wgrad_early(1)
    combine((3,), 4)
    wgrad(0)
    wgrad(1)

    with phase("hid"):
        swap_h().wait_recv()
        for core in range(2):
            @pl.when(c == core)
            def _():
                all_o[2 * FEAT:, HH * core:HH * (core + 1)] = hid2[64 * core:64 * core + 64, :]
                all_o[2 * FEAT:, HH * (1 - core):HH * (2 - core)] = hidr[...]

    with phase("retwait"):
        for a in parts:
            for k in NEAR:
                ys = (y + k) % NY
                for t in range(2):
                    if k > 0 or t > 0:
                        blk = ret.at[packed_rows(a, 2 * ys + (p if t == 0 else 1 - p)), :]
                        send(blk, blk, rts.at[a, 0, t], rtr.at[a, ys, t], partner, fi).wait_recv()
    with phase("unpack"):
        gt_o[...] = lax.dot_general(
            ret[...], pick[...], TN, preferred_element_type=F32
        ).astype(BF16)

    swap_gh(0).wait_send()
    swap_h().wait_send()
    for a in parts:
        for k in range(NY):
            for t in range(2):
                if k > 0 or t > 0:
                    dispatch(a, k, t).wait_send()
            forward(a, k).wait_send()
            trade(a, k).wait_send()
            share(a, k, z).wait_send()
        for q in range(SPLIT):
            for i in range(7):
                hop(a, i, q).wait_send()
            for k in range(4):
                long_hop(a, k, q).wait_send()
                if k < 3:
                    short_hop(a, k, q).wait_send()
        for leg in legs:
            for j, step, label in leg:
                d = chunk(step)
                to_partner(a, j, d).wait_send()
                give_back(a, j, d, 1).wait_send()

                @pl.when(d != y)
                def _():
                    give_back(a, j, d, 0).wait_send()


def on_device(tokens, counts, gate_values, up_values, gate_scales, up_scales, grad_hidden):
    vmem = pl.BlockSpec(memory_space=pltpu.VMEM)
    hbm = pl.BlockSpec(memory_space=pltpu.HBM)
    dma = pltpu.SemaphoreType.DMA
    slots = NX * NY * CAP
    packed_out, grad_tok = pl.pallas_call(
        body,
        out_shape=(
            jax.ShapeDtypeStruct((2 * FEAT + 64, HALF), BF16),
            jax.ShapeDtypeStruct((FEAT, 128), BF16),
        ),
        in_specs=[hbm] * 7,
        out_specs=(vmem, vmem),
        scratch_shapes=[
            pltpu.SMEM((1, EXPERTS), jnp.int32),
            pltpu.SMEM((8, 56), F32),
            pltpu.SMEM((8, 56), F32),
            pltpu.VMEM((FEAT, 128), BF16),
            pltpu.VMEM((64, HALF), BF16),
            pltpu.VMEM((EXPERTS * CAP, 128), BF16),
            pltpu.VMEM((EXPERTS * CAP, FEAT), BF16),
            pltpu.VMEM((slots, FEAT), BF16),
            pltpu.VMEM((FEAT, HALF), BF16),
            pltpu.VMEM((FEAT, HALF), BF16),
            pltpu.VMEM((2, FEAT, HALF), BF16),
            pltpu.VMEM((slots, HALF), F32),
            pltpu.VMEM((slots, HALF), BF16),
            pltpu.VMEM((slots, HALF), BF16),
            pltpu.VMEM((PARTS, 4, CH, HALF), BF16),
            pltpu.VMEM((PARTS, 4, CH, HALF), BF16),
            pltpu.VMEM((PARTS, 3, CH, HALF), BF16),
            pltpu.VMEM((PARTS, 3, CH, HALF), BF16),
            pltpu.VMEM((128, HH), BF16),
            pltpu.VMEM((128, HH), BF16),
            pltpu.VMEM((64, HH), BF16),
            pltpu.VMEM((2, slots, HALF), BF16),
            pltpu.VMEM((slots, FEAT), BF16),
            pltpu.VMEM((slots, FEAT), BF16),
            pltpu.VMEM((slots, FEAT), BF16),
            pltpu.VMEM((EXPERTS * CAP, FEAT), BF16),
            pltpu.VMEM((2, FEAT, HALF), F32),
            dma((7,)),
            dma((2,)),
            dma((2,)),
            dma((PARTS, NY, 2)),
            dma((PARTS, NY, 2)),
            dma((PARTS, NY)),
            dma((PARTS, NY)),
            dma((PARTS, NZ)),
            dma((PARTS, NZ)),
            dma((PARTS, 4, SPLIT)),
            dma((PARTS, 4, SPLIT)),
            dma((PARTS, 3, SPLIT)),
            dma((PARTS, 3, SPLIT)),
            dma((PARTS, 4, SPLIT)),
            dma((PARTS, 4, SPLIT)),
            dma((PARTS, 3, SPLIT)),
            dma((PARTS, 3, SPLIT)),
            dma((PARTS, NZ)),
            dma((PARTS, NZ)),
            dma((PARTS, NZ)),
            dma((PARTS, NZ)),
            dma((PARTS, NZ, 2)),
            dma((PARTS, NY, 2)),
        ],
        compiler_params=pltpu.CompilerParams(collective_id=0, has_side_effects=True, vmem_limit_bytes=40 << 20),
        name="moe",
    )(
        *(
            pltpu.with_memory_space_constraint(v, pltpu.HBM)
            for v in (
                tokens.T, counts, gate_values, up_values,
                gate_scales[0].T, up_scales[0].T, grad_hidden,
            )
        )
    )
    grad_gate = packed_out[None, :FEAT]
    grad_up = packed_out[None, FEAT:2 * FEAT]
    hidden = packed_out[None, 2 * FEAT:]
    return hidden, grad_gate, grad_up, grad_tok.T


def solution(mesh):
    in_specs = (
        P("expert", "fsdp"),
        P("expert", None),
        P("expert", "fsdp", None),
        P("expert", "fsdp", None),
        P("expert", None, None),
        P("expert", None, None),
        P("expert", "fsdp", None),
    )
    out_specs = (
        P("expert", "fsdp", None),
        P("expert", "fsdp", None),
        P("expert", "fsdp", None),
        P("expert", "fsdp"),
    )
    return jax.shard_map(
        on_device, mesh=mesh, in_specs=in_specs, out_specs=out_specs, check_vma=False
    )
```
